32 devices in a mesh: section: 4 (over y, x), expert: 8 (over z, core).
Axes of the slice: x: 2, y: 2, z: 4, core: 2. Of those that a mesh axis runs over, the one named last changes fastest.
Arguments:
- forward_input: bfloat16 [4, 576, 4096], P('section', 'expert'), may hold values from -6 to 6
- backward_cotangent: bfloat16 [4, 576, 4096], P('section', 'expert'), may hold values from -6 to 6
- saved_input: bfloat16 [4, 576, 4096], P('section', 'expert'), may hold values from -6 to 6
- saved_hidden: bfloat16 [4, 8, 360, 1536], P('section', 'expert'), may hold values from -8 to 8
- norm_gain: float32 [4, 4096], P('section'), may hold values from 0.5 to 2
- forward_experts: int32 [4, 576, 4], P('section', 'expert'), may hold values from 0 to 7, all different within a row; in each aligned block of 72 rows (0 to 71, 72 to 143, ..., all dimensions but the last counted through in order) at most 45 rows name the same one
- forward_gates: float32 [4, 576, 4], P('section', 'expert'), may hold values from 0.05 to 1
- backward_experts: int32 [4, 576, 4], P('section', 'expert'), may hold values from 0 to 7, all different within a row; in each aligned block of 72 rows (0 to 71, 72 to 143, ..., all dimensions but the last counted through in order) at most 45 rows name the same one
- backward_gates: float32 [4, 576, 4], P('section', 'expert'), may hold values from 0.05 to 1
- gate_up_weight: bfloat16 [4, 8, 4096, 1536], P('section', 'expert'), may hold values from -0.09375 to 0.09375
- down_weight: bfloat16 [4, 8, 768, 4096], P('section', 'expert'), may hold values from -0.21875 to 0.21875
Outputs:
- forward_output: bfloat16 [4, 576, 4096], P('section', 'expert')
- input_gradient: bfloat16 [4, 576, 4096], P('section', 'expert')
The draws below stay inside these ranges and needn't reach their ends.
Inputs may be any that keep to these rules, and one draw needn't show every extreme that they name: `forward_experts`: each token names 4 distinct experts. In the rows of one device (aligned blocks of 72 tokens) no expert is named by more than 45 entries, and in some device's rows some expert is named by exactly 45. `backward_experts`: same law as forward_experts, drawn independently.
All inputs are finite; a program needn't handle non-finite values.
Results may differ from the reference program's by a relative error of at most 0.0054.
Values may be sent and summed in bfloat16 or wider, within the bound.
A program may use at most 128 MiB of HBM per device.

```python
import math
import jax
import jax.numpy as jnp
import numpy as np
from jax import lax

D = 4096
FW = 768
TOK_DEV = 72
EXPERTS = 8
TOP = 4
CAP = 45
SLOTS = 360
TOKS = 576
SECTIONS = 4
N_SECTION = 4


def block_levels(rng, dims, cuts, low, high):
    def one(axis_at, shards_of):
        steps = jax.random.uniform(jax.random.fold_in(jax.random.fold_in(rng, 6), axis_at), (shards_of,), jnp.float32, low / len(cuts), high / len(cuts))
        return jnp.repeat(jnp.exp(steps), dims[axis_at] // shards_of).reshape((-1,) + (1,) * (len(dims) - axis_at - 1))

    factor_of = one(*cuts[0])
    for cut in cuts[1:]:
        factor_of = factor_of * one(*cut)
    return factor_of


def assign_block(key, own, number, rows, count, top, most, slope):
    ranking = jax.random.permutation(key, count)
    heavy_load, ordinary = shares(count, rows * top, most, slope, True), shares(count, rows * top, most, slope, False)
    places = jnp.arange(count)

    def named(lengths, offset_by):
        used = int((lengths > 0).sum())
        fixed = max(1, used // 4)
        moved = fixed + (places - fixed + offset_by * (used - fixed)) % max(1, count - fixed)
        return jnp.zeros((count,), jnp.int32).at[ranking[jnp.where(places < fixed, places, moved)]].set(jnp.asarray(lengths, jnp.int32))

    lengths = jnp.where(number % 4 == 0, named(heavy_load, number // 4), named(ordinary, number - number // 4 - 1))
    mixed = jax.random.permutation(jax.random.fold_in(own, 3), count)
    donor, taker = mixed[0:count // 2 * 2:2], mixed[1:count // 2 * 2:2]
    margin = jnp.minimum(lengths[donor] - 1, most - lengths[taker]) // 2
    margin = jnp.where((donor == ranking[0]) | (taker == ranking[0]) | (lengths[taker] == 0), 0, jnp.maximum(margin, 0))
    moved = jax.random.randint(jax.random.fold_in(own, 4), (count // 2,), 0, 1 << 20) % (margin + 1)
    lengths = lengths.at[donor].add(-moved).at[taker].add(moved)
    labels = jnp.searchsorted(jnp.cumsum(lengths), jnp.arange(rows * top), side="right").astype(jnp.int32)
    listing = labels.reshape(top, rows).T
    listing = listing[jax.random.permutation(jax.random.fold_in(own, 1), rows)]
    offset_by = jax.random.randint(jax.random.fold_in(own, 2), (rows, 1), 0, top)
    return jnp.take_along_axis(listing, (jnp.arange(top)[None, :] + offset_by) % top, axis=1)


def shares(count, total, most, skew, full):
    loads = [(1 << 20) // math.isqrt(grade ** skew) + 1 for grade in range(1, count + 1)]
    largest = most if full else min(most, max(-(-total // count), total * loads[0] // sum(loads)))
    least = 1 if total - largest >= count - 1 else 0
    holding, rest = [largest] + [least] * (count - 1), total - largest - least * (count - 1)
    while rest > 0:
        movable = [i for i in range(1, count) if holding[i] < largest] or [i for i in range(1, count) if holding[i] < most]
        mass, remaining = sum([loads[i] for i in movable]), rest
        for i in movable:
            more = min(most - holding[i], max(1, remaining * loads[i] // mass), rest)
            holding[i] = holding[i] + more
            rest = rest - more
    return np.array(holding)


def normal_values(key, extent, width, reach, pieces=(), held_as=jnp.bfloat16):
    drawn = jax.random.normal(key, extent, jnp.float32) * width
    if len(pieces) > 0:
        drawn = block_levels(key, extent, pieces, -0.22, 0.18) * drawn
    return jnp.clip(drawn, min=-reach, max=reach).astype(held_as)


def setup_inputs(seed: int = 0) -> dict:
    arg_keys = jax.random.split(jax.random.key(seed), 12)
    forward_input = normal_values(arg_keys[0], (SECTIONS, TOKS, D), 1.0, 6.0, ((0, 4), (1, 8)))
    backward_cotangent = normal_values(arg_keys[1], (SECTIONS, TOKS, D), 1.0, 6.0, ((0, 4), (1, 8)))
    saved_input = normal_values(arg_keys[2], (SECTIONS, TOKS, D), 1.0, 6.0, ((0, 4), (1, 8)))
    saved_hidden = normal_values(arg_keys[3], (SECTIONS, EXPERTS, SLOTS, 2 * FW), 1.5, 8.0, ((0, 4), (1, 8)))
    norm_gain = jnp.clip(jnp.exp(math.log(2.0) - 1.3862944 * jax.random.uniform(arg_keys[4], (SECTIONS, D), jnp.float32) ** block_levels(arg_keys[4], (SECTIONS, D), ((0, 4),), -0.2, 0.2)), 0.5, 2.0)
    forward_experts_keys = jax.random.split(jax.random.fold_in(arg_keys[5], 1), SECTIONS * TOKS // TOK_DEV)
    forward_experts_turns = jax.random.permutation(jax.random.fold_in(arg_keys[5], 3), SECTIONS * TOKS // TOK_DEV)
    forward_experts = jax.vmap(lambda own, number: assign_block(jax.random.fold_in(arg_keys[5], 2), own, number, TOK_DEV, EXPERTS, TOP, CAP, 2))(forward_experts_keys, forward_experts_turns).reshape((SECTIONS, TOKS, TOP))
    forward_gates = jnp.clip(jnp.exp(math.log(1.0) - 2.9957323 * jax.random.uniform(arg_keys[6], (SECTIONS, TOKS, TOP), jnp.float32) ** block_levels(arg_keys[6], (SECTIONS, TOKS, TOP), ((0, 4), (1, 8)), -0.2, 0.2)), 0.05, 1.0)
    backward_experts_keys = jax.random.split(jax.random.fold_in(arg_keys[7], 1), SECTIONS * TOKS // TOK_DEV)
    backward_experts_turns = jax.random.permutation(jax.random.fold_in(arg_keys[7], 3), SECTIONS * TOKS // TOK_DEV)
    backward_experts = jax.vmap(lambda own, number: assign_block(jax.random.fold_in(arg_keys[7], 2), own, number, TOK_DEV, EXPERTS, TOP, CAP, 2))(backward_experts_keys, backward_experts_turns).reshape((SECTIONS, TOKS, TOP))
    backward_gates = jnp.clip(jnp.exp(math.log(1.0) - 2.9957323 * jax.random.uniform(arg_keys[8], (SECTIONS, TOKS, TOP), jnp.float32) ** block_levels(arg_keys[8], (SECTIONS, TOKS, TOP), ((0, 4), (1, 8)), -0.2, 0.2)), 0.05, 1.0)
    gate_up_weight = normal_values(arg_keys[9], (SECTIONS, EXPERTS, D, 2 * FW), D ** -0.5, 0.09375, ((0, 4), (1, 8)))
    down_weight = normal_values(arg_keys[10], (SECTIONS, EXPERTS, FW, D), FW ** -0.5, 0.21875, ((0, 4), (1, 8)))
    return dict(forward_input=forward_input, backward_cotangent=backward_cotangent, saved_input=saved_input, saved_hidden=saved_hidden, norm_gain=norm_gain, forward_experts=forward_experts, forward_gates=forward_gates, backward_experts=backward_experts, backward_gates=backward_gates, gate_up_weight=gate_up_weight, down_weight=down_weight)


EPSILON = 1e-06

def norm_scale(values, gain_row):
    widened = values.astype(jnp.float32)
    inverse = lax.rsqrt(lax.optimization_barrier(jnp.mean(widened * widened, axis=-1, keepdims=True)) + EPSILON)
    return widened * inverse * gain_row

def normalized(gate_values):
    return gate_values / lax.optimization_barrier(jnp.sum(gate_values, axis=-1, keepdims=True))

def slot_of(expert_ids, expert_count):
    flat_ids = expert_ids.reshape(-1).astype(jnp.int32)
    onehot = (flat_ids[:, None] == jnp.arange(expert_count, dtype=jnp.int32)[None, :]).astype(jnp.int32)
    rank_table = jnp.cumsum(onehot, axis=0) - 1
    slot_index = lax.optimization_barrier(jnp.sum(rank_table * onehot, axis=1)).astype(jnp.int32)
    return (slot_index, flat_ids)

def global_rows(expert_ids):
    blocks = expert_ids.reshape(EXPERTS, TOK_DEV * TOP)

    def one_block(block_ids):
        return slot_of(block_ids, EXPERTS)
    slot_index, flat_ids = jax.vmap(one_block)(blocks)
    block_index = jnp.arange(EXPERTS, dtype=jnp.int32)[:, None]
    row_index = flat_ids * SLOTS + block_index * CAP + slot_index
    return row_index.reshape(-1).astype(jnp.int32)

def expert_forward(inputs, weight_in, weight_down):
    hidden_width = weight_down.shape[0]
    projected = jnp.dot(inputs, weight_in, preferred_element_type=jnp.float32)
    hidden = (jax.nn.silu(projected[:, :hidden_width]) * projected[:, hidden_width:]).astype(jnp.bfloat16)
    return jnp.dot(hidden, weight_down, preferred_element_type=jnp.float32).astype(jnp.bfloat16)

def expert_backward(cotangent_rows, saved_rows, weight_in, weight_down):
    hidden_width = weight_down.shape[0]
    grad_hidden = lax.dot_general(cotangent_rows, weight_down, (((1,), (1,)), ((), ())), preferred_element_type=jnp.float32)
    gate_value = saved_rows[:, :hidden_width].astype(jnp.float32)
    upward = saved_rows[:, hidden_width:].astype(jnp.float32)
    sigmoid_gate = jax.nn.sigmoid(gate_value)
    grad_gate = grad_hidden * upward * sigmoid_gate * (1.0 + gate_value * (1.0 - sigmoid_gate))
    grad_upper = grad_hidden * gate_value * sigmoid_gate
    grad_both = jnp.concatenate([grad_gate, grad_upper], axis=1).astype(jnp.bfloat16)
    return lax.dot_general(grad_both, weight_in, (((1,), (1,)), ((), ())), preferred_element_type=jnp.float32).astype(jnp.bfloat16)

def reference(forward_input, backward_cotangent, saved_input, saved_hidden, norm_gain, forward_experts, forward_gates, backward_experts, backward_gates, gate_up_weight, down_weight):
    outputs = []
    gradients = []
    for position in range(N_SECTION):
        source = max(position - 1, 0)
        gain_row = norm_gain[position].astype(jnp.float32)
        layer_in = forward_input[source]
        normed = norm_scale(layer_in, gain_row).astype(jnp.bfloat16)
        row_index = global_rows(forward_experts[position])
        buffer = jnp.zeros((EXPERTS * SLOTS, D), jnp.bfloat16).at[row_index].set(jnp.repeat(normed, TOP, axis=0))

        def serve_forward(operands):
            return expert_forward(operands[0], operands[1], operands[2])
        served = lax.map(serve_forward, (buffer.reshape(EXPERTS, SLOTS, D), gate_up_weight[position], down_weight[position]))
        picked = served.reshape(EXPERTS * SLOTS, D)[row_index].reshape(TOKS, TOP, D)
        mixture = jnp.einsum('tk,tkd->td', normalized(forward_gates[position]), picked.astype(jnp.float32))
        outputs.append((layer_in.astype(jnp.float32) + mixture).astype(jnp.bfloat16))
        cotangent = backward_cotangent[source]
        back_rows = global_rows(backward_experts[position])
        scaled = (normalized(backward_gates[position])[:, :, None] * cotangent.astype(jnp.float32)[:, None, :]).astype(jnp.bfloat16)
        buffer_back = jnp.zeros((EXPERTS * SLOTS, D), jnp.bfloat16).at[back_rows].set(scaled.reshape(-1, D))

        def serve_backward(operands):
            return expert_backward(operands[0], operands[1], operands[2], operands[3])
        returned = lax.map(serve_backward, (buffer_back.reshape(EXPERTS, SLOTS, D), saved_hidden[position], gate_up_weight[position], down_weight[position]))
        gathered = returned.reshape(EXPERTS * SLOTS, D)[back_rows].reshape(TOKS, TOP, D)
        grad_normed = lax.optimization_barrier(jnp.sum(gathered.astype(jnp.float32), axis=1))

        def apply_norm(inputs):
            return norm_scale(inputs, gain_row)
        primal, pullback = jax.vjp(apply_norm, saved_input[position].astype(jnp.float32))
        gradients.append((cotangent.astype(jnp.float32) + pullback(grad_normed)[0]).astype(jnp.bfloat16))
    return (jnp.stack(outputs), jnp.stack(gradients))
```

```python
import jax
import jax.numpy as jnp
from jax import lax
from jax.sharding import PartitionSpec as P

EPSILON = 1e-06


def passed_along(value, axis, steps):
    count = lax.axis_size(axis)
    initial, last = (max(0, -steps), min(count, count - steps))
    return lax.ppermute(value, axis, [(source, source + steps) for source in range(initial, last)])


def norm_scale(values, gain_row):
    widened = values.astype(jnp.float32)
    inverse = lax.rsqrt(jnp.mean(widened * widened, axis=-1, keepdims=True) + EPSILON)
    return widened * inverse * gain_row


def dense_weights(expert_ids, gates, expert_count):
    weights = gates / jnp.sum(gates, axis=-1, keepdims=True)
    onehot = expert_ids[:, :, None] == jnp.arange(expert_count, dtype=jnp.int32)[None, None, :]
    return jnp.sum(jnp.where(onehot, weights[:, :, None], 0.0), axis=1)


def local(
    forward_input,
    backward_cotangent,
    saved_input,
    saved_hidden,
    norm_gain,
    forward_experts,
    forward_gates,
    backward_experts,
    backward_gates,
    gate_up_weight,
    down_weight,
):
    peer_count = lax.axis_size("expert")
    me = lax.axis_index("expert")
    table = jnp.concatenate(
        [
            dense_weights(forward_experts[0], forward_gates[0], peer_count),
            dense_weights(backward_experts[0], backward_gates[0], peer_count),
        ],
        axis=1,
    )
    tables = lax.all_gather(table, "expert", axis=0, tiled=True)
    weight_f = lax.dynamic_slice_in_dim(tables, me, 1, axis=1)
    weight_b = lax.dynamic_slice_in_dim(tables, peer_count + me, 1, axis=1)

    moved_input, moved_cotangent = passed_along((forward_input, backward_cotangent), "section", 1)
    is_first = lax.axis_index("section") == 0
    layer_in = jnp.where(is_first, forward_input, moved_input)[0]
    cotangent = jnp.where(is_first, backward_cotangent, moved_cotangent)[0]
    token_count = layer_in.shape[0]
    slot_total = saved_hidden.shape[2]
    capacity = slot_total // peer_count
    gain_row = norm_gain[0]
    weight_in = gate_up_weight[0, 0]
    weight_down = down_weight[0, 0]
    hidden_width = weight_down.shape[0]

    normed = norm_scale(layer_in, gain_row).astype(jnp.bfloat16)
    all_normed = lax.all_gather(normed, "expert", axis=0, tiled=True)
    all_cotangent = lax.all_gather(cotangent, "expert", axis=0, tiled=True)

    projected = jnp.dot(all_normed, weight_in, preferred_element_type=jnp.float32)
    hidden = (jax.nn.silu(projected[:, :hidden_width]) * projected[:, hidden_width:]).astype(
        jnp.bfloat16
    )
    served = jnp.dot(hidden, weight_down, preferred_element_type=jnp.float32)
    served = (served * weight_f).astype(jnp.bfloat16)
    mixture = lax.psum_scatter(served, "expert", scatter_dimension=0, tiled=True)
    forward_output = (layer_in.astype(jnp.float32) + mixture.astype(jnp.float32)).astype(
        jnp.bfloat16
    )

    routed = (weight_b > 0.0).reshape(peer_count, token_count)
    slot = jnp.cumsum(routed.astype(jnp.int32), axis=1) - 1
    spread = (
        (slot[:, :, None] == jnp.arange(capacity, dtype=jnp.int32)[None, None, :])
        & routed[:, :, None]
    ).astype(jnp.bfloat16)
    saved = jnp.einsum(
        "jts,jsf->jtf",
        spread,
        saved_hidden[0, 0].reshape(peer_count, capacity, -1),
        preferred_element_type=jnp.float32,
    ).reshape(peer_count * token_count, -1)
    scaled = (weight_b * all_cotangent.astype(jnp.float32)).astype(jnp.bfloat16)
    grad_hidden = lax.dot_general(
        scaled, weight_down, (((1,), (1,)), ((), ())), preferred_element_type=jnp.float32
    )
    gate, up = saved[:, :hidden_width], saved[:, hidden_width:]
    sig = jax.nn.sigmoid(gate)
    grad_both = jnp.concatenate(
        [grad_hidden * up * sig * (1.0 + gate * (1.0 - sig)), grad_hidden * gate * sig], axis=1
    ).astype(jnp.bfloat16)
    grads = lax.dot_general(
        grad_both, weight_in, (((1,), (1,)), ((), ())), preferred_element_type=jnp.float32
    ).astype(jnp.bfloat16)
    grad_normed = lax.psum_scatter(grads, "expert", scatter_dimension=0, tiled=True).astype(
        jnp.float32
    )

    def apply_norm(inputs):
        return norm_scale(inputs, gain_row)

    primal, pullback = jax.vjp(apply_norm, saved_input[0].astype(jnp.float32))
    input_gradient = (cotangent.astype(jnp.float32) + pullback(grad_normed)[0]).astype(jnp.bfloat16)
    return (forward_output[None], input_gradient[None])


def solution(mesh):
    row = P("section", "expert", None)
    block = P("section", "expert", None, None)
    in_specs = (row, row, row, block, P("section", None), row, row, row, row, block, block)
    return jax.shard_map(
        local, mesh=mesh, in_specs=in_specs, out_specs=(row, row), check_vma=False
    )
```

```python
import functools

import jax
import jax.numpy as jnp
from jax import lax
from jax.experimental import pallas as pl
from jax.experimental.pallas import tpu as pltpu
from jax.sharding import PartitionSpec as P

EPSILON = 1e-06


def passed_along(value, axis, steps):
    count = lax.axis_size(axis)
    initial, last = (max(0, -steps), min(count, count - steps))
    return lax.ppermute(value, axis, [(source, source + steps) for source in range(initial, last)])


def norm_scale(values, gain_row):
    widened = values.astype(jnp.float32)
    inverse = lax.rsqrt(jnp.mean(widened * widened, axis=-1, keepdims=True) + EPSILON)
    return widened * inverse * gain_row


def dense_weights(expert_ids, gates, expert_count):
    weights = gates / jnp.sum(gates, axis=-1, keepdims=True)
    onehot = expert_ids[:, :, None] == jnp.arange(expert_count, dtype=jnp.int32)[None, None, :]
    return jnp.sum(jnp.where(onehot, weights[:, :, None], 0.0), axis=1)


def local_plain(
    forward_input,
    backward_cotangent,
    saved_input,
    saved_hidden,
    norm_gain,
    forward_experts,
    forward_gates,
    backward_experts,
    backward_gates,
    gate_up_weight,
    down_weight,
):
    peer_count = lax.axis_size("expert")
    me = lax.axis_index("expert")
    table = jnp.concatenate(
        [
            dense_weights(forward_experts[0], forward_gates[0], peer_count),
            dense_weights(backward_experts[0], backward_gates[0], peer_count),
        ],
        axis=1,
    )
    tables = lax.all_gather(table, "expert", axis=0, tiled=True)
    weight_f = lax.dynamic_slice_in_dim(tables, me, 1, axis=1)
    weight_b = lax.dynamic_slice_in_dim(tables, peer_count + me, 1, axis=1)

    moved_input, moved_cotangent = passed_along((forward_input, backward_cotangent), "section", 1)
    is_first = lax.axis_index("section") == 0
    layer_in = jnp.where(is_first, forward_input, moved_input)[0]
    cotangent = jnp.where(is_first, backward_cotangent, moved_cotangent)[0]
    token_count = layer_in.shape[0]
    slot_total = saved_hidden.shape[2]
    capacity = slot_total // peer_count
    gain_row = norm_gain[0]
    weight_in = gate_up_weight[0, 0]
    weight_down = down_weight[0, 0]
    hidden_width = weight_down.shape[0]

    normed = norm_scale(layer_in, gain_row).astype(jnp.bfloat16)
    all_normed = lax.all_gather(normed, "expert", axis=0, tiled=True)
    all_cotangent = lax.all_gather(cotangent, "expert", axis=0, tiled=True)

    projected = jnp.dot(all_normed, weight_in, preferred_element_type=jnp.float32)
    hidden = (jax.nn.silu(projected[:, :hidden_width]) * projected[:, hidden_width:]).astype(
        jnp.bfloat16
    )
    served = jnp.dot(hidden, weight_down, preferred_element_type=jnp.float32)
    served = (served * weight_f).astype(jnp.bfloat16)
    mixture = lax.psum_scatter(served, "expert", scatter_dimension=0, tiled=True)
    forward_output = (layer_in.astype(jnp.float32) + mixture.astype(jnp.float32)).astype(
        jnp.bfloat16
    )

    routed = (weight_b > 0.0).reshape(peer_count, token_count)
    slot = jnp.cumsum(routed.astype(jnp.int32), axis=1) - 1
    spread = (
        (slot[:, :, None] == jnp.arange(capacity, dtype=jnp.int32)[None, None, :])
        & routed[:, :, None]
    ).astype(jnp.bfloat16)
    saved = jnp.einsum(
        "jts,jsf->jtf",
        spread,
        saved_hidden[0, 0].reshape(peer_count, capacity, -1),
        preferred_element_type=jnp.float32,
    ).reshape(peer_count * token_count, -1)
    scaled = (weight_b * all_cotangent.astype(jnp.float32)).astype(jnp.bfloat16)
    grad_hidden = lax.dot_general(
        scaled, weight_down, (((1,), (1,)), ((), ())), preferred_element_type=jnp.float32
    )
    gate, up = saved[:, :hidden_width], saved[:, hidden_width:]
    sig = jax.nn.sigmoid(gate)
    grad_both = jnp.concatenate(
        [grad_hidden * up * sig * (1.0 + gate * (1.0 - sig)), grad_hidden * gate * sig], axis=1
    ).astype(jnp.bfloat16)
    grads = lax.dot_general(
        grad_both, weight_in, (((1,), (1,)), ((), ())), preferred_element_type=jnp.float32
    ).astype(jnp.bfloat16)
    grad_normed = lax.psum_scatter(grads, "expert", scatter_dimension=0, tiled=True).astype(
        jnp.float32
    )

    def apply_norm(inputs):
        return norm_scale(inputs, gain_row)

    primal, pullback = jax.vjp(apply_norm, saved_input[0].astype(jnp.float32))
    input_gradient = (cotangent.astype(jnp.float32) + pullback(grad_normed)[0]).astype(jnp.bfloat16)
    return (forward_output[None], input_gradient[None])


VMEM_LIMIT = 60 * 1024 * 1024
CHUNKS = 4
LANES = 128


def relay_kernel(
    sections, chips, tokens, width, hidden, capacity,
    fin_ref, cot_ref, saved_ref, gain_ref, table_ref, stored_ref, win_hbm, wdown_hbm,
    out_ref, grad_ref,
    win, wdown, ct, xs, own_cot, layer, tables, wf, wb, proj, both, slots_b, slots_f, chain_b, chain_f, acc,
    w_sem, t_send, t_recv, sh_send, sh_recv,
    b_right, b_left, b_sib, b_recv, b_srecv,
    f_right, f_left, f_sib, f_recv, f_srecv,
    zb_send, zb_recv, zb_ss, zb_sr,
    zf_send, zf_recv, zf_ss, zf_sr,
):
    peers = 2 * chips
    section = lax.axis_index("section")
    me = lax.axis_index("expert")
    chip, core = me // 2, me % 2
    sibling = chip * 2 + 1 - core
    right = jnp.minimum(me + 2, peers - 1)
    left = jnp.maximum(me - 2, 0)
    cols = width // CHUNKS
    base = core * chips
    other = (1 - core) * chips
    mine = base + chip
    has_left, has_right = chip > 0, chip < chips - 1

    def span(k):
        return pl.ds(pl.multiple_of(k * cols, LANES), cols)

    def expert_copy(src, dst, send, recv, peer):
        return pltpu.make_async_remote_copy(
            src_ref=src, dst_ref=dst, send_sem=send, recv_sem=recv,
            device_id={"expert": peer}, device_id_type=pl.DeviceIdType.MESH,
        )

    barrier = pltpu.get_barrier_semaphore()
    for step in range(1, peers):
        pl.semaphore_signal(
            barrier, inc=1, device_id={"expert": lax.rem(me + step, peers)},
            device_id_type=pl.DeviceIdType.MESH,
        )

    @pl.when(section > 0)
    def _():
        pl.semaphore_signal(barrier, inc=1, device_id={"section": section - 1}, device_id_type=pl.DeviceIdType.MESH)

    @pl.when(section < sections - 1)
    def _():
        pl.semaphore_signal(barrier, inc=1, device_id={"section": section + 1}, device_id_type=pl.DeviceIdType.MESH)

    arrivals = jnp.where(section > 0, 1, 0) + jnp.where(section < sections - 1, 1, 0)
    pl.semaphore_wait(barrier, arrivals + peers - 1)

    following = jnp.minimum(section + 1, sections - 1)

    def shift_cot(k):
        return pltpu.make_async_remote_copy(
            src_ref=cot_ref.at[:, span(k)], dst_ref=ct.at[mine, :, span(k)],
            send_sem=sh_send.at[k], recv_sem=sh_recv.at[k],
            device_id={"section": following}, device_id_type=pl.DeviceIdType.MESH,
        )

    shift_in = pltpu.make_async_remote_copy(
        src_ref=fin_ref, dst_ref=layer, send_sem=sh_send.at[CHUNKS], recv_sem=sh_recv.at[CHUNKS],
        device_id={"section": following}, device_id_type=pl.DeviceIdType.MESH,
    )

    @pl.when(section < sections - 1)
    def _():
        for k in range(CHUNKS):
            shift_cot(k).start()
        shift_in.start()

    copy_down = pltpu.make_async_copy(wdown_hbm, wdown, w_sem.at[0])
    copy_in = pltpu.make_async_copy(win_hbm, win, w_sem.at[1])
    copy_down.start()
    copy_in.start()

    def table_copy(step):
        peer = lax.rem(me + step, peers)
        return expert_copy(table_ref, tables.at[mine], t_send.at[step], t_recv.at[step], peer)

    for step in range(1, peers):
        table_copy(step).start()

    @pl.when(section == 0)
    def _():
        ct[mine] = cot_ref[...]
        layer[...] = fin_ref[...]

    tables[mine] = table_ref[...]

    def gather_copies(buf, sems, block, k):
        s_right, s_left, s_sib, recv, s_recv = sems
        view = buf.at[base + block, :, span(k)]
        return (
            expert_copy(view, view, s_right.at[block, k], recv.at[block, k], right),
            expert_copy(view, view, s_left.at[block, k], recv.at[block, k], left),
            expert_copy(view, view, s_sib.at[block, k], s_recv.at[block, k], sibling),
        )

    def sibling_arrival(buf, sems, block, k):
        s_sib, s_recv = sems[2], sems[4]
        view = buf.at[other + block, :, span(k)]
        return expert_copy(view, view, s_sib.at[block, k], s_recv.at[block, k], sibling)

    def gather_own(buf, sems, k):
        to_right, to_left, to_sib = gather_copies(buf, sems, chip, k)

        @pl.when(has_right)
        def _():
            to_right.start()

        @pl.when(has_left)
        def _():
            to_left.start()

        to_sib.start()

    def gather_relay(buf, sems, k):
        for hop in range(1, chips):
            @pl.when(chip >= hop)
            def _():
                to_right, _, to_sib = gather_copies(buf, sems, chip - hop, k)
                to_right.wait_recv()

                @pl.when(has_right)
                def _():
                    to_right.start()

                to_sib.start()

            @pl.when(chip + hop < chips)
            def _():
                _, to_left, to_sib = gather_copies(buf, sems, chip + hop, k)
                to_left.wait_recv()

                @pl.when(has_left)
                def _():
                    to_left.start()

                to_sib.start()

        for block in range(chips):
            sibling_arrival(buf, sems, block, k).wait_recv()

    def gather_drain(buf, sems, k):
        for block in range(chips):
            to_right, to_left, to_sib = gather_copies(buf, sems, block, k)

            @pl.when(has_right & (block <= chip))
            def _():
                to_right.wait_send()

            @pl.when(has_left & (block >= chip))
            def _():
                to_left.wait_send()

            to_sib.wait_send()

    def cross_copy(buf, slots, sems, k):
        return expert_copy(
            buf.at[pl.ds(other, chips), :, span(k)], slots.at[:, :, span(k)],
            sems[2].at[k], sems[3].at[k], sibling,
        )

    def chain_copy(buf, chain, sems, dest, slot, k, peer):
        return expert_copy(
            buf.at[base + dest, :, span(k)], chain.at[slot, :, span(k)],
            sems[0].at[dest, k], sems[1].at[slot, k], peer,
        )

    def chain_step(buf, slots, chain, sems, hop, k):
        def advance(dest, slot, source_exists, peer):
            value = buf[base + dest, :, span(k)].astype(jnp.float32) + slots[
                dest, :, span(k)
            ].astype(jnp.float32)
            buf[base + dest, :, span(k)] = value.astype(jnp.bfloat16)

            @pl.when(source_exists)
            def _():
                chain_copy(buf, chain, sems, dest, slot, k, peer).wait_recv()
                buf[base + dest, :, span(k)] = (
                    value + chain[slot, :, span(k)].astype(jnp.float32)
                ).astype(jnp.bfloat16)

            chain_copy(buf, chain, sems, dest, slot, k, peer).start()

        @pl.when(chip <= hop)
        def _():
            dest = chips - 1 - hop + chip
            advance(dest, dest + 1, has_left, right)

        @pl.when(chips - 1 - chip <= hop)
        def _():
            dest = hop - (chips - 1 - chip)
            advance(dest, dest, has_right, left)

    def chain_end(buf, slots, chain, sems, k):
        total = acc.at[0 if buf is ct else 1]
        total[:, span(k)] = buf[mine, :, span(k)].astype(jnp.float32) + slots[
            chip, :, span(k)
        ].astype(jnp.float32)

        @pl.when(has_left)
        def _():
            chain_copy(buf, chain, sems, chip, chip + 1, k, right).wait_recv()
            total[:, span(k)] += chain[chip + 1, :, span(k)].astype(jnp.float32)

        @pl.when(has_right)
        def _():
            chain_copy(buf, chain, sems, chip, chip, k, left).wait_recv()
            total[:, span(k)] += chain[chip, :, span(k)].astype(jnp.float32)

    def chain_round(buf, slots, chain, sems, step):
        for hop in range(chips):
            k = step - hop

            @pl.when((k >= 0) & (k < CHUNKS))
            def _():
                if hop == 0:
                    cross_copy(buf, slots, sems, k).wait_recv()
                if hop < chips - 1:
                    chain_step(buf, slots, chain, sems, hop, k)
                else:
                    chain_end(buf, slots, chain, sems, k)

    def chain_drain(buf, slots, chain, sems, k):
        cross_copy(buf, slots, sems, k).wait_send()
        for dest in range(chips):
            @pl.when(chip != dest)
            def _():
                chain_copy(buf, chain, sems, dest, dest, k, left).wait_send()

    def loop(count, body):
        def wrapped(k, carry):
            body(k)
            return carry

        lax.fori_loop(0, count, wrapped, 0)

    back = (b_right, b_left, b_sib, b_recv, b_srecv)
    ahead = (f_right, f_left, f_sib, f_recv, f_srecv)
    back_sum = (zb_send, zb_recv, zb_ss, zb_sr)
    ahead_sum = (zf_send, zf_recv, zf_ss, zf_sr)

    def first(k):
        @pl.when(section > 0)
        def _():
            shift_cot(k).wait_recv()

        gather_own(ct, back, k)

    loop(CHUNKS, first)

    @pl.when(section > 0)
    def _():
        shift_in.wait_recv()

    widened = layer[...].astype(jnp.float32)
    inverse = lax.rsqrt(jnp.mean(widened * widened, axis=-1, keepdims=True) + EPSILON)
    xs[mine] = (widened * inverse * gain_ref[...]).astype(jnp.bfloat16)
    own_cot[...] = ct[mine]

    for step in range(1, peers):
        table_copy(step).wait_recv()
    lane = lax.broadcasted_iota(jnp.int32, (tokens, LANES), 1)
    for block in range(peers):
        values = tables[block]
        rows = pl.ds(block * tokens, tokens)
        wf[rows, :] = jnp.sum(jnp.where(lane == me, values, 0.0), axis=1, keepdims=True)
        wb[rows, :] = jnp.sum(jnp.where(lane == me + peers, values, 0.0), axis=1, keepdims=True)

    copy_down.wait()

    def widen(buf, k):
        return jnp.concatenate(
            [buf[block, :, span(k)].astype(jnp.float32) for block in range(peers)], axis=0
        )

    def spread(buf, k, value):
        for block in range(peers):
            buf[block, :, span(k)] = value[block * tokens : (block + 1) * tokens].astype(
                jnp.bfloat16
            )

    def gather_back(k):
        gather_relay(ct, back, k)
        scaled = (widen(ct, k) * wb[...]).astype(jnp.bfloat16)
        part = lax.dot_general(
            scaled, wdown[:, span(k)], (((1,), (1,)), ((), ())), preferred_element_type=jnp.float32
        )

        @pl.when(k == 0)
        def _():
            proj[:, :hidden] = part

        @pl.when(k > 0)
        def _():
            proj[:, :hidden] += part

    loop(CHUNKS, gather_back)
    gather_own(xs, ahead, 0)
    loop(CHUNKS, functools.partial(gather_drain, ct, back))

    lower = (
        lax.broadcasted_iota(jnp.int32, (tokens, tokens), 1)
        < lax.broadcasted_iota(jnp.int32, (tokens, tokens), 0)
    ).astype(jnp.bfloat16)
    slot_total = stored_ref.shape[0]
    place = lax.broadcasted_iota(jnp.int32, (tokens, slot_total), 1).astype(jnp.float32)

    def hidden_grads(block):
        rows = pl.ds(pl.multiple_of(block * tokens, 8), tokens)
        routed = wb[rows, :] > 0.0
        marks = jnp.where(routed, 1.0, 0.0)
        wide_marks = jnp.broadcast_to(marks, (tokens, LANES)).astype(jnp.bfloat16)
        rank = jnp.dot(lower, wide_marks, preferred_element_type=jnp.float32)[:, :1]
        source = (block % chips) * 2 + block // chips
        slot = rank + (source * capacity).astype(jnp.float32)
        pick = jnp.where((place == slot) & (marks > 0.0), 1.0, 0.0).astype(jnp.bfloat16)
        stored = jnp.dot(pick, stored_ref[...], preferred_element_type=jnp.float32)
        gate, up = stored[:, :hidden], stored[:, hidden:]
        grad_hidden = proj[rows, :hidden]
        sig = jax.nn.sigmoid(gate)
        both[block, :, :hidden] = (
            grad_hidden * up * sig * (1.0 + gate * (1.0 - sig))
        ).astype(jnp.bfloat16)
        both[block, :, hidden:] = (grad_hidden * gate * sig).astype(jnp.bfloat16)

    loop(peers, hidden_grads)
    copy_in.wait()

    def all_rows():
        return jnp.concatenate(
            [both[block].astype(jnp.float32) for block in range(peers)], axis=0
        ).astype(jnp.bfloat16)

    def middle(k):
        @pl.when(k + 1 < CHUNKS)
        def _():
            gather_own(xs, ahead, k + 1)

        rows = pl.ds(pl.multiple_of(k * cols, LANES), cols)
        spread(
            ct, k,
            lax.dot_general(
                all_rows(), win[rows, :], (((1,), (1,)), ((), ())),
                preferred_element_type=jnp.float32,
            ),
        )
        cross_copy(ct, slots_b, back_sum, k).start()
        gather_relay(xs, ahead, k)
        chain_round(ct, slots_b, chain_b, back_sum, k)
        part = jnp.dot(
            widen(xs, k).astype(jnp.bfloat16), win[rows, :], preferred_element_type=jnp.float32
        )

        @pl.when(k == 0)
        def _():
            proj[...] = part

        @pl.when(k > 0)
        def _():
            proj[...] += part

    loop(CHUNKS, middle)
    loop(CHUNKS, functools.partial(gather_drain, xs, ahead))

    def activate(block):
        rows = pl.ds(pl.multiple_of(block * tokens, 8), tokens)
        gate, up = proj[rows, :hidden], proj[rows, hidden:]
        both[block, :, :hidden] = (gate / (1.0 + jnp.exp(-gate)) * up).astype(jnp.bfloat16)

    loop(peers, activate)

    def serve(k):
        active = jnp.concatenate(
            [both[block, :, :hidden].astype(jnp.float32) for block in range(peers)], axis=0
        ).astype(jnp.bfloat16)
        value = jnp.dot(active, wdown[:, span(k)], preferred_element_type=jnp.float32)
        spread(xs, k, value * wf[...])
        cross_copy(xs, slots_f, ahead_sum, k).start()
        chain_round(xs, slots_f, chain_f, ahead_sum, k)

        @pl.when(k + CHUNKS < CHUNKS + chips - 1)
        def _():
            chain_round(ct, slots_b, chain_b, back_sum, k + CHUNKS)

    loop(CHUNKS, serve)
    for step in range(2 * CHUNKS, CHUNKS + chips - 1):
        chain_round(ct, slots_b, chain_b, back_sum, step)

    saved = saved_ref[...].astype(jnp.float32)
    inverse = lax.rsqrt(jnp.mean(saved * saved, axis=-1, keepdims=True) + EPSILON)
    pulled = acc[0] * gain_ref[...]
    along = jnp.mean(saved * pulled, axis=-1, keepdims=True)
    grad_ref[...] = (
        own_cot[...].astype(jnp.float32) + inverse * (pulled - saved * (inverse * inverse * along))
    ).astype(jnp.bfloat16)

    def last(step):
        chain_round(xs, slots_f, chain_f, ahead_sum, step + CHUNKS)

    loop(chips - 1, last)
    out_ref[...] = (layer[...].astype(jnp.float32) + acc[1]).astype(jnp.bfloat16)

    loop(CHUNKS, functools.partial(chain_drain, ct, slots_b, chain_b, back_sum))
    loop(CHUNKS, functools.partial(chain_drain, xs, slots_f, chain_f, ahead_sum))
    for step in range(1, peers):
        table_copy(step).wait_send()

    @pl.when(section < sections - 1)
    def _():
        for k in range(CHUNKS):
            shift_cot(k).wait_send()
        shift_in.wait_send()


def local_fused(
    forward_input,
    backward_cotangent,
    saved_input,
    saved_hidden,
    norm_gain,
    forward_experts,
    forward_gates,
    backward_experts,
    backward_gates,
    gate_up_weight,
    down_weight,
):
    peers = lax.axis_size("expert")
    chips = peers // 2
    tokens, width = forward_input.shape[1:]
    hidden = down_weight.shape[2]
    slot_total = saved_hidden.shape[2]
    table = jnp.concatenate(
        [
            dense_weights(forward_experts[0], forward_gates[0], peers),
            dense_weights(backward_experts[0], backward_gates[0], peers),
            jnp.zeros((tokens, LANES - 2 * peers), jnp.float32),
        ],
        axis=1,
    )
    rows = peers * tokens
    bf16, f32 = jnp.bfloat16, jnp.float32
    dma = pltpu.SemaphoreType.DMA
    gather_sems = [dma((chips, CHUNKS))] * 5
    sum_sems = [dma((chips, CHUNKS)), dma((chips + 1, CHUNKS)), dma((CHUNKS,)), dma((CHUNKS,))]
    vmem = pl.BlockSpec(memory_space=pltpu.VMEM)
    hbm = pl.BlockSpec(memory_space=pl.ANY)
    out = jax.ShapeDtypeStruct((tokens, width), bf16)
    forward_output, input_gradient = pl.pallas_call(
        functools.partial(
            relay_kernel, lax.axis_size("section"), chips, tokens, width, hidden, slot_total // peers
        ),
        out_shape=(out, out),
        in_specs=[vmem] * 6 + [hbm] * 2,
        out_specs=(vmem, vmem),
        scratch_shapes=[
            pltpu.VMEM((width, 2 * hidden), bf16),
            pltpu.VMEM((hidden, width), bf16),
            pltpu.VMEM((peers, tokens, width), bf16),
            pltpu.VMEM((peers, tokens, width), bf16),
            pltpu.VMEM((tokens, width), bf16),
            pltpu.VMEM((tokens, width), bf16),
            pltpu.VMEM((peers, tokens, LANES), f32),
            pltpu.VMEM((rows, 1), f32),
            pltpu.VMEM((rows, 1), f32),
            pltpu.VMEM((rows, 2 * hidden), f32),
            pltpu.VMEM((peers, tokens, 2 * hidden), bf16),
            pltpu.VMEM((chips, tokens, width), bf16),
            pltpu.VMEM((chips, tokens, width), bf16),
            pltpu.VMEM((chips + 1, tokens, width), bf16),
            pltpu.VMEM((chips + 1, tokens, width), bf16),
            pltpu.VMEM((2, tokens, width), f32),
            dma((2,)),
            dma((peers,)),
            dma((peers,)),
            dma((CHUNKS + 1,)),
            dma((CHUNKS + 1,)),
        ]
        + gather_sems + gather_sems + sum_sems + sum_sems,
        compiler_params=pltpu.CompilerParams(
            collective_id=0, has_side_effects=True, vmem_limit_bytes=VMEM_LIMIT
        ),
    )(
        forward_input[0], backward_cotangent[0], saved_input[0], norm_gain, table,
        saved_hidden[0, 0], gate_up_weight[0, 0], down_weight[0, 0],
    )
    return (forward_output[None], input_gradient[None])


def local(*arrays):
    peers = lax.axis_size("expert")
    tokens, width = arrays[0].shape[1:]
    hidden = arrays[10].shape[2]
    weights = 6 * hidden * width
    buffers = (2 * peers + 2 * (peers + 1)) * tokens * width * 2
    fits = weights + buffers < VMEM_LIMIT * 3 // 4
    return (local_fused if fits and peers % 2 == 0 else local_plain)(*arrays)


def solution(mesh):
    row = P("section", "expert", None)
    block = P("section", "expert", None, None)
    in_specs = (row, row, row, block, P("section", None), row, row, row, row, block, block)
    return jax.shard_map(
        local, mesh=mesh, in_specs=in_specs, out_specs=(row, row), check_vma=False
    )
```

```python
import functools

import jax
import jax.numpy as jnp
from jax import lax
from jax.experimental import pallas as pl
from jax.experimental.pallas import tpu as pltpu
from jax.sharding import PartitionSpec as P

EPSILON = 1e-06


def passed_along(value, axis, steps):
    count = lax.axis_size(axis)
    initial, last = (max(0, -steps), min(count, count - steps))
    return lax.ppermute(value, axis, [(source, source + steps) for source in range(initial, last)])


def norm_scale(values, gain_row):
    widened = values.astype(jnp.float32)
    inverse = lax.rsqrt(jnp.mean(widened * widened, axis=-1, keepdims=True) + EPSILON)
    return widened * inverse * gain_row


def dense_weights(expert_ids, gates, expert_count):
    weights = gates / jnp.sum(gates, axis=-1, keepdims=True)
    onehot = expert_ids[:, :, None] == jnp.arange(expert_count, dtype=jnp.int32)[None, None, :]
    return jnp.sum(jnp.where(onehot, weights[:, :, None], 0.0), axis=1)


def local_plain(
    forward_input,
    backward_cotangent,
    saved_input,
    saved_hidden,
    norm_gain,
    forward_experts,
    forward_gates,
    backward_experts,
    backward_gates,
    gate_up_weight,
    down_weight,
):
    peer_count = lax.axis_size("expert")
    me = lax.axis_index("expert")
    table = jnp.concatenate(
        [
            dense_weights(forward_experts[0], forward_gates[0], peer_count),
            dense_weights(backward_experts[0], backward_gates[0], peer_count),
        ],
        axis=1,
    )
    tables = lax.all_gather(table, "expert", axis=0, tiled=True)
    weight_f = lax.dynamic_slice_in_dim(tables, me, 1, axis=1)
    weight_b = lax.dynamic_slice_in_dim(tables, peer_count + me, 1, axis=1)

    moved_input, moved_cotangent = passed_along((forward_input, backward_cotangent), "section", 1)
    is_first = lax.axis_index("section") == 0
    layer_in = jnp.where(is_first, forward_input, moved_input)[0]
    cotangent = jnp.where(is_first, backward_cotangent, moved_cotangent)[0]
    token_count = layer_in.shape[0]
    slot_total = saved_hidden.shape[2]
    capacity = slot_total // peer_count
    gain_row = norm_gain[0]
    weight_in = gate_up_weight[0, 0]
    weight_down = down_weight[0, 0]
    hidden_width = weight_down.shape[0]

    normed = norm_scale(layer_in, gain_row).astype(jnp.bfloat16)
    all_normed = lax.all_gather(normed, "expert", axis=0, tiled=True)
    all_cotangent = lax.all_gather(cotangent, "expert", axis=0, tiled=True)

    projected = jnp.dot(all_normed, weight_in, preferred_element_type=jnp.float32)
    hidden = (jax.nn.silu(projected[:, :hidden_width]) * projected[:, hidden_width:]).astype(
        jnp.bfloat16
    )
    served = jnp.dot(hidden, weight_down, preferred_element_type=jnp.float32)
    served = (served * weight_f).astype(jnp.bfloat16)
    mixture = lax.psum_scatter(served, "expert", scatter_dimension=0, tiled=True)
    forward_output = (layer_in.astype(jnp.float32) + mixture.astype(jnp.float32)).astype(
        jnp.bfloat16
    )

    routed = (weight_b > 0.0).reshape(peer_count, token_count)
    slot = jnp.cumsum(routed.astype(jnp.int32), axis=1) - 1
    spread = (
        (slot[:, :, None] == jnp.arange(capacity, dtype=jnp.int32)[None, None, :])
        & routed[:, :, None]
    ).astype(jnp.bfloat16)
    saved = jnp.einsum(
        "jts,jsf->jtf",
        spread,
        saved_hidden[0, 0].reshape(peer_count, capacity, -1),
        preferred_element_type=jnp.float32,
    ).reshape(peer_count * token_count, -1)
    scaled = (weight_b * all_cotangent.astype(jnp.float32)).astype(jnp.bfloat16)
    grad_hidden = lax.dot_general(
        scaled, weight_down, (((1,), (1,)), ((), ())), preferred_element_type=jnp.float32
    )
    gate, up = saved[:, :hidden_width], saved[:, hidden_width:]
    sig = jax.nn.sigmoid(gate)
    grad_both = jnp.concatenate(
        [grad_hidden * up * sig * (1.0 + gate * (1.0 - sig)), grad_hidden * gate * sig], axis=1
    ).astype(jnp.bfloat16)
    grads = lax.dot_general(
        grad_both, weight_in, (((1,), (1,)), ((), ())), preferred_element_type=jnp.float32
    ).astype(jnp.bfloat16)
    grad_normed = lax.psum_scatter(grads, "expert", scatter_dimension=0, tiled=True).astype(
        jnp.float32
    )

    def apply_norm(inputs):
        return norm_scale(inputs, gain_row)

    primal, pullback = jax.vjp(apply_norm, saved_input[0].astype(jnp.float32))
    input_gradient = (cotangent.astype(jnp.float32) + pullback(grad_normed)[0]).astype(jnp.bfloat16)
    return (forward_output[None], input_gradient[None])


VMEM_LIMIT = 60 * 1024 * 1024
CHUNKS = 4
LANES = 128


def relay_kernel(
    sections, chips, tokens, width, hidden, capacity,
    fin_ref, cot_ref, saved_ref, gain_ref, fid_ref, fgate_ref, bid_ref, bgate_ref, stored_ref, win_hbm, wdown_hbm,
    out_ref, grad_ref,
    win, wdown, pool, own_cot, layer, table_ref, tables, wf, wb, proj, both, slots_b, slots_f, chain_b, chain_f, acc,
    w_sem, t_send, t_recv, sh_send, sh_recv,
    s_right, s_left, s_sib, g_recv, g_srecv,
    zb_send, zb_recv, zb_ss, zb_sr,
    zf_send, zf_recv, zf_ss, zf_sr,
):
    peers = 2 * chips
    section = lax.axis_index("section")
    me = lax.axis_index("expert")
    chip, core = me // 2, me % 2
    sibling = chip * 2 + 1 - core
    right = jnp.minimum(me + 2, peers - 1)
    left = jnp.maximum(me - 2, 0)
    cols = width // CHUNKS
    base = core * chips
    other = (1 - core) * chips
    mine = base + chip
    has_left, has_right = chip > 0, chip < chips - 1
    ct, xs = pool.at[pl.ds(0, peers)], pool.at[pl.ds(peers, peers)]

    def span(k):
        return pl.ds(pl.multiple_of(k * cols, LANES), cols)

    def expert_copy(src, dst, send, recv, peer):
        return pltpu.make_async_remote_copy(
            src_ref=src, dst_ref=dst, send_sem=send, recv_sem=recv,
            device_id={"expert": peer}, device_id_type=pl.DeviceIdType.MESH,
        )

    barrier = pltpu.get_barrier_semaphore()
    for step in range(1, peers):
        pl.semaphore_signal(
            barrier, inc=1, device_id={"expert": lax.rem(me + step, peers)},
            device_id_type=pl.DeviceIdType.MESH,
        )

    @pl.when(section > 0)
    def _():
        pl.semaphore_signal(barrier, inc=1, device_id={"section": section - 1}, device_id_type=pl.DeviceIdType.MESH)

    @pl.when(section < sections - 1)
    def _():
        pl.semaphore_signal(barrier, inc=1, device_id={"section": section + 1}, device_id_type=pl.DeviceIdType.MESH)

    arrivals = jnp.where(section > 0, 1, 0) + jnp.where(section < sections - 1, 1, 0)
    pl.semaphore_wait(barrier, arrivals + peers - 1)

    following = jnp.minimum(section + 1, sections - 1)

    def shift_cot(k):
        return pltpu.make_async_remote_copy(
            src_ref=cot_ref.at[:, span(k)], dst_ref=ct.at[mine, :, span(k)],
            send_sem=sh_send.at[k], recv_sem=sh_recv.at[k],
            device_id={"section": following}, device_id_type=pl.DeviceIdType.MESH,
        )

    shift_in = pltpu.make_async_remote_copy(
        src_ref=fin_ref, dst_ref=layer, send_sem=sh_send.at[CHUNKS], recv_sem=sh_recv.at[CHUNKS],
        device_id={"section": following}, device_id_type=pl.DeviceIdType.MESH,
    )

    @pl.when(section < sections - 1)
    def _():
        for k in range(CHUNKS):
            shift_cot(k).start()

    copy_down = pltpu.make_async_copy(wdown_hbm, wdown, w_sem.at[0])
    copy_in = pltpu.make_async_copy(win_hbm, win, w_sem.at[1])
    copy_down.start()
    copy_in.start()

    lane = lax.broadcasted_iota(jnp.int32, (tokens, LANES), 1)

    def dense(ids, gates, offset):
        weights = gates / jnp.sum(gates, axis=-1, keepdims=True)
        total = jnp.zeros((tokens, LANES), jnp.float32)
        for choice in range(ids.shape[1]):
            hit = lane == ids[:, choice : choice + 1] + offset
            total += jnp.where(hit, weights[:, choice : choice + 1], 0.0)
        return total

    table_ref[...] = dense(fid_ref[...], fgate_ref[...], 0) + dense(
        bid_ref[...], bgate_ref[...], peers
    )

    def table_copy(step):
        peer = lax.rem(me + step, peers)
        return expert_copy(table_ref, tables.at[mine], t_send.at[step], t_recv.at[step], peer)

    for step in range(1, peers):
        table_copy(step).start()

    @pl.when(section == 0)
    def _():
        ct[mine] = cot_ref[...]
        layer[...] = fin_ref[...]

    tables[mine] = table_ref[...]

    def gather_copies(index, block):
        which, k = index // CHUNKS, index % CHUNKS
        view = pool.at[which * peers + base + block, :, span(k)]
        recv = g_recv.at[which, block, k]
        return (
            expert_copy(view, view, s_right.at[which, block, k], recv, right),
            expert_copy(view, view, s_left.at[which, block, k], recv, left),
            expert_copy(
                view, view, s_sib.at[which, block, k], g_srecv.at[which, block, k], sibling
            ),
        )

    def gather_own(index):
        to_right, to_left, to_sib = gather_copies(index, chip)

        @pl.when(has_right)
        def _():
            to_right.start()

        @pl.when(has_left)
        def _():
            to_left.start()

        to_sib.start()

    def gather_hop(index, hop):
        @pl.when(chip >= hop)
        def _():
            to_right, _, to_sib = gather_copies(index, chip - hop)
            to_right.wait_recv()

            @pl.when(has_right)
            def _():
                to_right.start()

            to_sib.start()

        @pl.when(chip + hop < chips)
        def _():
            _, to_left, to_sib = gather_copies(index, chip + hop)
            to_left.wait_recv()

            @pl.when(has_left)
            def _():
                to_left.start()

            to_sib.start()

    def gather_round(step):
        for hop in range(chips - 1, 0, -1):
            index = step - hop + 1

            @pl.when((index >= 0) & (index < 2 * CHUNKS))
            def _():
                gather_hop(index, hop)

    def gather_end(index):
        which, k = index // CHUNKS, index % CHUNKS
        for block in range(chips):
            view = pool.at[which * peers + other + block, :, span(k)]
            expert_copy(
                view, view, s_sib.at[which, block, k], g_srecv.at[which, block, k], sibling
            ).wait_recv()

    def gather_drain(index):
        for block in range(chips):
            to_right, to_left, to_sib = gather_copies(index, block)

            @pl.when(has_right & (block <= chip))
            def _():
                to_right.wait_send()

            @pl.when(has_left & (block >= chip))
            def _():
                to_left.wait_send()

            to_sib.wait_send()

    def cross_copy(buf, slots, sems, k):
        return expert_copy(
            buf.at[pl.ds(other, chips), :, span(k)], slots.at[:, :, span(k)],
            sems[2].at[k], sems[3].at[k], sibling,
        )

    def chain_copy(buf, chain, sems, dest, slot, k, peer):
        return expert_copy(
            buf.at[base + dest, :, span(k)], chain.at[slot, :, span(k)],
            sems[0].at[dest, k], sems[1].at[slot, k], peer,
        )

    def chain_step(buf, slots, chain, sems, hop, k):
        def advance(dest, slot, source_exists, peer):
            value = buf[base + dest, :, span(k)].astype(jnp.float32) + slots[
                dest, :, span(k)
            ].astype(jnp.float32)
            buf[base + dest, :, span(k)] = value.astype(jnp.bfloat16)

            @pl.when(source_exists)
            def _():
                chain_copy(buf, chain, sems, dest, slot, k, peer).wait_recv()
                buf[base + dest, :, span(k)] = (
                    value + chain[slot, :, span(k)].astype(jnp.float32)
                ).astype(jnp.bfloat16)

            chain_copy(buf, chain, sems, dest, slot, k, peer).start()

        @pl.when(chip <= hop)
        def _():
            dest = chips - 1 - hop + chip
            advance(dest, dest + 1, has_left, right)

        @pl.when(chips - 1 - chip <= hop)
        def _():
            dest = hop - (chips - 1 - chip)
            advance(dest, dest, has_right, left)

    def chain_end(buf, slots, chain, sems, k):
        total = acc.at[0 if sems is back_sum else 1]
        total[:, span(k)] = buf[mine, :, span(k)].astype(jnp.float32) + slots[
            chip, :, span(k)
        ].astype(jnp.float32)

        @pl.when(has_left)
        def _():
            chain_copy(buf, chain, sems, chip, chip + 1, k, right).wait_recv()
            total[:, span(k)] += chain[chip + 1, :, span(k)].astype(jnp.float32)

        @pl.when(has_right)
        def _():
            chain_copy(buf, chain, sems, chip, chip, k, left).wait_recv()
            total[:, span(k)] += chain[chip, :, span(k)].astype(jnp.float32)

    def chain_round(buf, slots, chain, sems, step):
        for hop in range(chips - 1, -1, -1):
            k = step - hop

            @pl.when((k >= 0) & (k < CHUNKS))
            def _():
                if hop == 0:
                    cross_copy(buf, slots, sems, k).wait_recv()
                if hop < chips - 1:
                    chain_step(buf, slots, chain, sems, hop, k)
                else:
                    chain_end(buf, slots, chain, sems, k)

    def chain_drain(buf, slots, chain, sems, k):
        cross_copy(buf, slots, sems, k).wait_send()
        for dest in range(chips):
            @pl.when(chip != dest)
            def _():
                chain_copy(buf, chain, sems, dest, dest, k, left).wait_send()

    def loop(count, body):
        def wrapped(k, carry):
            body(k)
            return carry

        lax.fori_loop(0, count, wrapped, 0)

    back_sum = (zb_send, zb_recv, zb_ss, zb_sr)
    ahead_sum = (zf_send, zf_recv, zf_ss, zf_sr)

    def first(k):
        @pl.when(section > 0)
        def _():
            shift_cot(k).wait_recv()

        gather_own(k)

    lead = 2
    span_rounds = chips - 2
    loop(lead, first)

    for step in range(1, peers):
        table_copy(step).wait_recv()
    for block in range(peers):
        values = tables[block]
        rows = pl.ds(block * tokens, tokens)
        wf[rows, :] = jnp.sum(jnp.where(lane == me, values, 0.0), axis=1, keepdims=True)
        wb[rows, :] = jnp.sum(jnp.where(lane == me + peers, values, 0.0), axis=1, keepdims=True)

    @pl.when(section < sections - 1)
    def _():
        shift_in.start()

    def opening(step):
        first(step + lead)
        gather_round(step)

    loop(CHUNKS - lead, opening)

    @pl.when(section > 0)
    def _():
        shift_in.wait_recv()

    widened = layer[...].astype(jnp.float32)
    inverse = lax.rsqrt(jnp.mean(widened * widened, axis=-1, keepdims=True) + EPSILON)
    xs[mine] = (widened * inverse * gain_ref[...]).astype(jnp.bfloat16)
    own_cot[...] = ct[mine]

    copy_down.wait()

    def widen(buf, k):
        return jnp.concatenate(
            [buf[block, :, span(k)].astype(jnp.float32) for block in range(peers)], axis=0
        )

    def spread(buf, k, value):
        for block in range(peers):
            buf[block, :, span(k)] = value[block * tokens : (block + 1) * tokens].astype(
                jnp.bfloat16
            )

    def gather_back(k):
        @pl.when(k < CHUNKS)
        def _():
            gather_own(k + CHUNKS)

        gather_round(k + CHUNKS - lead)
        ready = k + CHUNKS - lead - span_rounds

        @pl.when((ready >= 0) & (ready < CHUNKS))
        def _():
            gather_end(ready)
            hidden_part(ready)

    def hidden_part(k):
        scaled = (widen(ct, k) * wb[...]).astype(jnp.bfloat16)
        part = lax.dot_general(
            scaled, wdown[:, span(k)], (((1,), (1,)), ((), ())), preferred_element_type=jnp.float32
        )

        @pl.when(k == 0)
        def _():
            proj[:, :hidden] = part

        @pl.when(k > 0)
        def _():
            proj[:, :hidden] += part

    opened = max(CHUNKS, lead + span_rounds)
    loop(opened, gather_back)
    loop(CHUNKS, gather_drain)

    lower = (
        lax.broadcasted_iota(jnp.int32, (tokens, tokens), 1)
        < lax.broadcasted_iota(jnp.int32, (tokens, tokens), 0)
    ).astype(jnp.bfloat16)
    slot_total = stored_ref.shape[0]
    place = lax.broadcasted_iota(jnp.int32, (tokens, slot_total), 1).astype(jnp.float32)

    def hidden_grads(block):
        rows = pl.ds(pl.multiple_of(block * tokens, 8), tokens)
        routed = wb[rows, :] > 0.0
        marks = jnp.where(routed, 1.0, 0.0)
        wide_marks = jnp.broadcast_to(marks, (tokens, LANES)).astype(jnp.bfloat16)
        rank = jnp.dot(lower, wide_marks, preferred_element_type=jnp.float32)[:, :1]
        source = (block % chips) * 2 + block // chips
        slot = rank + (source * capacity).astype(jnp.float32)
        pick = jnp.where((place == slot) & (marks > 0.0), 1.0, 0.0).astype(jnp.bfloat16)
        stored = jnp.dot(pick, stored_ref[...], preferred_element_type=jnp.float32)
        gate, up = stored[:, :hidden], stored[:, hidden:]
        grad_hidden = proj[rows, :hidden]
        sig = jax.nn.sigmoid(gate)
        both[block, :, :hidden] = (
            grad_hidden * up * sig * (1.0 + gate * (1.0 - sig))
        ).astype(jnp.bfloat16)
        both[block, :, hidden:] = (grad_hidden * gate * sig).astype(jnp.bfloat16)

    loop(peers, hidden_grads)
    copy_in.wait()

    def all_rows():
        return jnp.concatenate(
            [both[block].astype(jnp.float32) for block in range(peers)], axis=0
        ).astype(jnp.bfloat16)

    def middle(k):
        rows = pl.ds(pl.multiple_of(k * cols, LANES), cols)
        spread(
            ct, k,
            lax.dot_general(
                all_rows(), win[rows, :], (((1,), (1,)), ((), ())),
                preferred_element_type=jnp.float32,
            ),
        )
        cross_copy(ct, slots_b, back_sum, k).start()
        gather_round(k + opened + CHUNKS - lead)
        chain_round(ct, slots_b, chain_b, back_sum, k)
        gather_end(k + CHUNKS)
        part = jnp.dot(
            widen(xs, k).astype(jnp.bfloat16), win[rows, :], preferred_element_type=jnp.float32
        )

        @pl.when(k == 0)
        def _():
            proj[...] = part

        @pl.when(k > 0)
        def _():
            proj[...] += part

    loop(CHUNKS, middle)
    loop(CHUNKS, lambda k: gather_drain(k + CHUNKS))

    def activate(block):
        rows = pl.ds(pl.multiple_of(block * tokens, 8), tokens)
        gate, up = proj[rows, :hidden], proj[rows, hidden:]
        both[block, :, :hidden] = (gate / (1.0 + jnp.exp(-gate)) * up).astype(jnp.bfloat16)

    loop(peers, activate)

    def serve(k):
        active = jnp.concatenate(
            [both[block, :, :hidden].astype(jnp.float32) for block in range(peers)], axis=0
        ).astype(jnp.bfloat16)
        value = jnp.dot(active, wdown[:, span(k)], preferred_element_type=jnp.float32)
        spread(xs, k, value * wf[...])
        cross_copy(xs, slots_f, ahead_sum, k).start()
        chain_round(xs, slots_f, chain_f, ahead_sum, k)

        @pl.when(k + CHUNKS < CHUNKS + chips - 1)
        def _():
            chain_round(ct, slots_b, chain_b, back_sum, k + CHUNKS)

    loop(CHUNKS, serve)
    for step in range(2 * CHUNKS, CHUNKS + chips - 1):
        chain_round(ct, slots_b, chain_b, back_sum, step)

    saved = saved_ref[...].astype(jnp.float32)
    inverse = lax.rsqrt(jnp.mean(saved * saved, axis=-1, keepdims=True) + EPSILON)
    pulled = acc[0] * gain_ref[...]
    along = jnp.mean(saved * pulled, axis=-1, keepdims=True)
    grad_ref[...] = (
        own_cot[...].astype(jnp.float32) + inverse * (pulled - saved * (inverse * inverse * along))
    ).astype(jnp.bfloat16)

    def last(step):
        chain_round(xs, slots_f, chain_f, ahead_sum, step + CHUNKS)

    loop(chips - 1, last)
    out_ref[...] = (layer[...].astype(jnp.float32) + acc[1]).astype(jnp.bfloat16)

    loop(CHUNKS, functools.partial(chain_drain, ct, slots_b, chain_b, back_sum))
    loop(CHUNKS, functools.partial(chain_drain, xs, slots_f, chain_f, ahead_sum))
    for step in range(1, peers):
        table_copy(step).wait_send()

    @pl.when(section < sections - 1)
    def _():
        for k in range(CHUNKS):
            shift_cot(k).wait_send()
        shift_in.wait_send()


def local_fused(
    forward_input,
    backward_cotangent,
    saved_input,
    saved_hidden,
    norm_gain,
    forward_experts,
    forward_gates,
    backward_experts,
    backward_gates,
    gate_up_weight,
    down_weight,
):
    peers = lax.axis_size("expert")
    chips = peers // 2
    tokens, width = forward_input.shape[1:]
    hidden = down_weight.shape[2]
    slot_total = saved_hidden.shape[2]
    rows = peers * tokens
    bf16, f32 = jnp.bfloat16, jnp.float32
    dma = pltpu.SemaphoreType.DMA
    gather_sems = [dma((2, chips, CHUNKS))] * 5
    sum_sems = [dma((chips, CHUNKS)), dma((chips + 1, CHUNKS)), dma((CHUNKS,)), dma((CHUNKS,))]
    vmem = pl.BlockSpec(memory_space=pltpu.VMEM)
    hbm = pl.BlockSpec(memory_space=pl.ANY)
    out = jax.ShapeDtypeStruct((tokens, width), bf16)
    forward_output, input_gradient = pl.pallas_call(
        functools.partial(
            relay_kernel, lax.axis_size("section"), chips, tokens, width, hidden, slot_total // peers
        ),
        out_shape=(out, out),
        in_specs=[vmem] * 9 + [hbm] * 2,
        out_specs=(vmem, vmem),
        scratch_shapes=[
            pltpu.VMEM((width, 2 * hidden), bf16),
            pltpu.VMEM((hidden, width), bf16),
            pltpu.VMEM((2 * peers, tokens, width), bf16),
            pltpu.VMEM((tokens, width), bf16),
            pltpu.VMEM((tokens, width), bf16),
            pltpu.VMEM((tokens, LANES), f32),
            pltpu.VMEM((peers, tokens, LANES), f32),
            pltpu.VMEM((rows, 1), f32),
            pltpu.VMEM((rows, 1), f32),
            pltpu.VMEM((rows, 2 * hidden), f32),
            pltpu.VMEM((peers, tokens, 2 * hidden), bf16),
            pltpu.VMEM((chips, tokens, width), bf16),
            pltpu.VMEM((chips, tokens, width), bf16),
            pltpu.VMEM((chips + 1, tokens, width), bf16),
            pltpu.VMEM((chips + 1, tokens, width), bf16),
            pltpu.VMEM((2, tokens, width), f32),
            dma((2,)),
            dma((peers,)),
            dma((peers,)),
            dma((CHUNKS + 1,)),
            dma((CHUNKS + 1,)),
        ]
        + gather_sems + sum_sems + sum_sems,
        compiler_params=pltpu.CompilerParams(
            collective_id=0, has_side_effects=True, vmem_limit_bytes=VMEM_LIMIT
        ),
    )(
        forward_input[0], backward_cotangent[0], saved_input[0], norm_gain,
        forward_experts[0], forward_gates[0], backward_experts[0], backward_gates[0],
        saved_hidden[0, 0], gate_up_weight[0, 0], down_weight[0, 0],
    )
    return (forward_output[None], input_gradient[None])


def local(*arrays):
    peers = lax.axis_size("expert")
    tokens, width = arrays[0].shape[1:]
    hidden = arrays[10].shape[2]
    weights = 6 * hidden * width
    buffers = (2 * peers + 2 * (peers + 1)) * tokens * width * 2
    fits = weights + buffers < VMEM_LIMIT * 3 // 4
    return (local_fused if fits and peers % 2 == 0 else local_plain)(*arrays)


def solution(mesh):
    row = P("section", "expert", None)
    block = P("section", "expert", None, None)
    in_specs = (row, row, row, block, P("section", None), row, row, row, row, block, block)
    return jax.shard_map(
        local, mesh=mesh, in_specs=in_specs, out_specs=(row, row), check_vma=False
    )
```
